32 devices in a mesh: dp: 8 (over y, x, core), tensor: 4 (over z).
Axes of the slice: x: 2, y: 2, z: 4, core: 2. Of those that a mesh axis runs over, the one named last changes fastest.
Arguments:
- tokens: bfloat16 [4096, 2048], P('dp', 'tensor'), may hold values from -6 to 6
- cotangent: bfloat16 [4096, 2048], P('dp', 'tensor'), may hold values from -6 to 6
- src_of: int32 [4096], P('dp'), may hold values from 0 to 4095, as said below
- lengths: int32 [8, 6], P('dp'), may hold values from 1 to 256, 512 in all within a row
- norm1_gain: float32 [2048], replicated, may hold values from 0.25 to 1.75
- w_in: bfloat16 [3, 2048, 2048], P(None, None, 'tensor'), may hold values from -0.125 to 0.125
- conv_w: bfloat16 [3, 2048], P(None, 'tensor'), may hold values from -3.5 to 3.5
- w_out: bfloat16 [2048, 2048], P('tensor'), may hold values from -0.125 to 0.125
- norm2_gain: float32 [2048], replicated, may hold values from 0.25 to 1.75
- w_gate: bfloat16 [2048, 8192], P(None, 'tensor'), may hold values from -0.125 to 0.125
- w_up: bfloat16 [2048, 8192], P(None, 'tensor'), may hold values from -0.125 to 0.125
- w_down: bfloat16 [8192, 2048], P('tensor'), may hold values from -0.0625 to 0.0625
Outputs:
- mixed: float32 [4096, 2048], P('dp', 'tensor')
- token_grad: float32 [4096, 2048], P('dp', 'tensor')
- norm1_gain_grad: float32 [2048], P('dp')
- w_in_grad: float32 [3, 2048, 2048], P(None, 'dp', 'tensor')
- conv_w_grad: float32 [3, 2048], P(None, ('tensor', 'dp'))
- w_out_grad: float32 [2048, 2048], P('tensor', 'dp')
- norm2_gain_grad: float32 [2048], P('dp')
- w_gate_grad: float32 [2048, 8192], P('dp', 'tensor')
- w_up_grad: float32 [2048, 8192], P('dp', 'tensor')
- w_down_grad: float32 [8192, 2048], P('tensor', 'dp')
The draws below stay inside these ranges and needn't reach their ends.
Inputs may be any that keep to these rules, and one draw needn't show every extreme that they name: `src_of`: A permutation of all tokens. Of the 512 positions dealt to one index of dp, 64 take their tokens from each shard of dp but two; one shard gives 128 and one gives none. `lengths`: each row fills its index's 512 dealt positions.
All inputs are finite; a program needn't handle non-finite values.
Results may differ from the reference program's by a relative error of at most 0.0097.
Values may be sent and summed in bfloat16 or wider, within the bound.
No kernel may reach another device: no remote copies, remote signals or barrier semaphores. Data moves between devices by JAX's collectives and lax.ppermute only.
A program may use at most 320 MiB of HBM per device.

```python
import math
import jax
import jax.numpy as jnp
import numpy as np
from jax import lax

D = 2048
FF = 8192
CONV = 3
TOK_DEV = 512
NSEQ = 6
MOST = 256
TOKENS = 4096
N_DP = 8


def draw_src_of(key, part):
    groups = TOKENS // TOK_DEV
    share = TOK_DEV // groups
    key_order, key_rows, key_ties = jax.random.split(key, 3)
    order = jax.random.permutation(key_order, groups)
    following = jnp.roll(order, -1)
    devices = jnp.arange(groups, dtype=jnp.int32)
    extra = (devices[None, :] == order[:, None]).astype(jnp.int32) - (devices[None, :] == following[:, None]).astype(jnp.int32)
    counts = share + share * extra
    bounds = jnp.cumsum(counts, axis=0)
    local = jnp.arange(TOK_DEV, dtype=jnp.int32)
    dest_sorted = jnp.sum((bounds[:, :, None] <= local[None, None, :]).astype(jnp.int32), axis=0)
    dest_tokens = jax.random.permutation(key_rows, dest_sorted, axis=1, independent=True)
    scores = dest_tokens.reshape(-1) * TOKENS + jax.random.permutation(key_ties, TOKENS).astype(jnp.int32)
    return jnp.argsort(scores, stable=True).astype(jnp.int32)


def levels(key, extent, pieces, low, high):
    factor_of, own = 1.0, jax.random.fold_in(key, 6)
    for axis_at, blocks in pieces:
        steps = jnp.exp(jax.random.uniform(jax.random.fold_in(own, axis_at), (blocks,), jnp.float32, low / len(pieces), high / len(pieces)))
        factor_of = factor_of * jnp.repeat(steps, extent[axis_at] // blocks).reshape([-1 if axis == axis_at else 1 for axis in range(len(extent))])
    return factor_of


def split_up(amount, total, reach, slope):
    weights = [(1 << 20) // math.isqrt(rank ** slope) + 1 for rank in range(2, amount + 1)]
    surplus, given = total - reach - (amount - 1), [1] * (amount - 1)
    while surplus > 0:
        free = [i for i in range(amount - 1) if given[i] < reach]
        mass, left = sum([weights[i] for i in free]), surplus
        for i in free:
            more = min(reach - given[i], max(1, left * weights[i] // mass), surplus)
            given[i] = given[i] + more
            surplus = surplus - more
    return np.array([reach] + given)


def ragged(own_key, number_of, total, bound, skew):
    if number_of == 2:
        one = jax.random.randint(own_key, (), max(1, total - bound), min(bound, total - 1) + 1)
        return jnp.stack([one, total - one])
    tallies = jnp.asarray(split_up(number_of, total, bound, skew), jnp.int32)
    twos = (number_of - 1) // 2
    donor, taker = tallies[1:1 + 2 * twos:2], tallies[2:2 + 2 * twos:2]
    slack = jnp.minimum(donor - 1, bound - taker)
    moved = jax.random.randint(jax.random.fold_in(own_key, 1), (twos,), 0, 1 << 20) % (slack + 1)
    tallies = tallies.at[1:1 + 2 * twos:2].set(donor - moved).at[2:2 + 2 * twos:2].set(taker + moved)
    return tallies[jax.random.permutation(jax.random.fold_in(own_key, 2), number_of)]


def gaussian(key, extent, scale, most, cuts=(), held_as=jnp.bfloat16):
    entries = scale * jax.random.normal(key, extent, jnp.float32)
    if cuts:
        entries = entries * levels(key, extent, cuts, -0.22, 0.18)
    return jnp.clip(entries, -most, most).astype(held_as)


def setup_inputs(seed: int = 0) -> dict:
    seeds = jax.random.split(jax.random.key(seed), 13)
    tokens = gaussian(seeds[0], (TOKENS, D), 1.0, 6.0, ((0, 8), (1, 4)))
    cotangent = gaussian(seeds[1], (TOKENS, D), 1.0, 6.0, ((0, 8), (1, 4)))
    src_of = draw_src_of(jax.random.fold_in(seeds[12], 71), 0)
    lengths = jax.vmap(lambda own: ragged(own, NSEQ, TOK_DEV, MOST, 2))(jax.random.split(seeds[3], N_DP)).reshape((N_DP, NSEQ)).astype(jnp.int32)
    norm1_gain = jnp.clip(1.0 + 0.15 * jax.random.normal(seeds[4], (D,), jnp.float32), 0.25, 1.75)
    w_in = gaussian(seeds[5], (3, D, D), D ** -0.5, 0.125, ((2, 4),))
    conv_w = gaussian(seeds[6], (CONV, D), CONV ** -0.5, 3.5, ((1, 4),))
    w_out = gaussian(seeds[7], (D, D), D ** -0.5, 0.125, ((0, 4),))
    norm2_gain = jnp.clip(1.0 + 0.15 * jax.random.normal(seeds[8], (D,), jnp.float32), 0.25, 1.75)
    w_gate = gaussian(seeds[9], (D, FF), D ** -0.5, 0.125, ((1, 4),))
    w_up = gaussian(seeds[10], (D, FF), D ** -0.5, 0.125, ((1, 4),))
    w_down = gaussian(seeds[11], (FF, D), FF ** -0.5, 0.0625, ((0, 4),))
    return {"tokens": tokens, "cotangent": cotangent, "src_of": src_of, "lengths": lengths, "norm1_gain": norm1_gain, "w_in": w_in, "conv_w": conv_w, "w_out": w_out, "norm2_gain": norm2_gain, "w_gate": w_gate, "w_up": w_up, "w_down": w_down}


EPS = 1e-05
HIGH = lax.Precision.HIGHEST

@jax.custom_vjp
def low(v):
    return lax.optimization_barrier(v.astype(jnp.bfloat16)).astype(jnp.float32)

@jax.custom_vjp
def low_back(v):
    return v

def low_keep(v):
    return (low(v), None)

def low_pass(kept, grad):
    return (grad,)

def back_keep(v):
    return (v, None)

def back_low(kept, grad):
    return (low(grad),)
low.defvjp(low_keep, low_pass)
low_back.defvjp(back_keep, back_low)

def shifted(values, steps):
    padding = jnp.zeros((steps, values.shape[1]), values.dtype)
    return jnp.concatenate([padding, values[:-steps]], axis=0)

def block_forward(params, inputs, first, second):
    norm1_gain, w_in, conv_w, w_out, norm2_gain, w_gate, w_up, w_down = params
    scale_one = lax.rsqrt(lax.optimization_barrier(jnp.mean(inputs * inputs, axis=-1, keepdims=True)) + EPS)
    normed_one = low(inputs * scale_one * norm1_gain)
    projected = low_back(jnp.einsum('td,kde->kte', normed_one, w_in, precision=HIGH))
    b_gate = projected[0]
    c_gate = projected[1]
    values = projected[2]
    gated = b_gate * values
    convolved = conv_w[0] * shifted(gated, 2) * second + conv_w[1] * shifted(gated, 1) * first + conv_w[2] * gated
    mixed_in = low(c_gate * convolved)
    branch = low_back(jnp.dot(mixed_in, w_out, precision=HIGH))
    resid = inputs + branch
    scale_two = lax.rsqrt(lax.optimization_barrier(jnp.mean(resid * resid, axis=-1, keepdims=True)) + EPS)
    normed_two = low(resid * scale_two * norm2_gain)
    gate = low_back(jnp.dot(normed_two, w_gate, precision=HIGH))
    up_proj = low_back(jnp.dot(normed_two, w_up, precision=HIGH))
    hidden = low(jax.nn.silu(gate) * up_proj)
    return resid + low_back(jnp.dot(hidden, w_down, precision=HIGH))

def reference(tokens, cotangent, src_of, lengths, norm1_gain, w_in, conv_w, w_out, norm2_gain, w_gate, w_up, w_down):
    total = tokens.shape[0]
    groups = lengths.shape[0]
    per_group = total // groups
    inputs = tokens[src_of].astype(jnp.float32)
    grad_out = cotangent[src_of].astype(jnp.float32)
    offsets = (jnp.arange(groups, dtype=jnp.int32) * per_group)[:, None]
    starts = (jnp.cumsum(lengths, axis=1) - lengths + offsets).astype(jnp.int32)
    marks = jnp.zeros((total,), jnp.float32).at[starts.reshape(-1)].set(1.0)
    first = 1.0 - marks
    earlier = jnp.concatenate([jnp.ones((1,), jnp.float32), marks[:-1]])
    second = first * (1.0 - earlier)
    params = tuple((item.astype(jnp.float32) for item in (norm1_gain, w_in, conv_w, w_out, norm2_gain, w_gate, w_up, w_down)))
    bunch = 4 if 4 * per_group <= 4352 else 1
    blocks = total // (bunch * per_group)
    rows = bunch * per_group
    width_all = inputs.shape[1]

    def one_block(carry, items):
        block_in, block_cot, block_first, block_second = items

        def forward(weights, acts):
            return block_forward(weights, acts, block_first, block_second)
        outputs, pull = jax.vjp(forward, params, block_in)
        weight_grads, input_grads = pull(block_cot)
        carry = jax.tree.map(lambda total_grad, part_grad: total_grad + part_grad, carry, weight_grads)
        return (carry, (outputs, input_grads))
    start_grads = tuple((jnp.zeros_like(item) for item in params))
    stacked = (inputs.reshape(blocks, rows, width_all), grad_out.reshape(blocks, rows, width_all), first.reshape(blocks, rows, 1), second.reshape(blocks, rows, 1))
    grads, (outputs, input_grads) = lax.scan(one_block, start_grads, stacked)
    dealt_out = outputs.reshape(total, width_all)
    dealt_grad = input_grads.reshape(total, width_all)
    mixed = jnp.zeros_like(dealt_out).at[src_of].set(dealt_out)
    token_grad = jnp.zeros_like(dealt_grad).at[src_of].set(dealt_grad)
    return (mixed, token_grad, grads[0], grads[1], grads[2], grads[3], grads[4], grads[5], grads[6], grads[7])
```

```python
import jax
import jax.numpy as jnp
import numpy as np
from jax import lax
from jax.sharding import PartitionSpec as P

EPS = 1e-05
F32 = jnp.float32
BF16 = jnp.bfloat16


def shifted(values, steps):
    padding = jnp.zeros((steps, values.shape[1]), values.dtype)
    return jnp.concatenate([padding, values[:-steps]], axis=0)


def raised(values, steps):
    padding = jnp.zeros((steps, values.shape[1]), values.dtype)
    return jnp.concatenate([values[steps:], padding], axis=0)


def inner_rows(left, right):
    return lax.dot_general(
        left, right, (((0,), (0,)), ((), ())), preferred_element_type=F32
    )


def outer_cols(left, right):
    return lax.dot_general(
        left, right, (((1,), (1,)), ((), ())), preferred_element_type=F32
    )


def ring_order(n):
    return list(range(0, n, 2)) + list(range(1, n, 2))[::-1]


def ring_shift(x):
    n = lax.axis_size("tensor")
    order = ring_order(n)
    return lax.ppermute(x, "tensor", [(order[i], order[(i + 1) % n]) for i in range(n)])


def ring_ids():
    n = lax.axis_size("tensor")
    order = ring_order(n)
    place = {a: i for i, a in enumerate(order)}
    table = np.array(
        [[order[(place[a] - s) % n] for s in range(n)] for a in range(n)], np.int32
    )
    row = jnp.asarray(table)[lax.axis_index("tensor")]
    return [row[s] for s in range(n)]


def gather_cols(x, ids):
    parts = [x]
    for _ in range(len(ids) - 1):
        x = ring_shift(x)
        parts.append(x)
    width = x.shape[1]
    out = jnp.zeros((x.shape[0], width * len(ids)), x.dtype)
    for s, part in enumerate(parts):
        out = lax.dynamic_update_slice_in_dim(out, part, ids[s] * width, 1)
    return out


def scatter_cols(partial, ids):
    n = len(ids)
    acc = partial(ids[1 % n]).astype(BF16)
    for s in range(1, n):
        moved = ring_shift(acc)
        acc = moved.astype(F32) + partial(ids[(s + 1) % n])
        if s < n - 1:
            acc = acc.astype(BF16)
    return acc


def total_tensor(x):
    n = lax.axis_size("tensor")
    out = x
    for k in range(1, n):
        out = out + lax.ppermute(x, "tensor", [(i, (i + k) % n) for i in range(n)])
    return out


def swap(x, mask):
    n = lax.axis_size("dp")
    return lax.ppermute(x, "dp", [(i, i ^ mask) for i in range(n)])


def relative_blocks(x, me, width):
    n = lax.axis_size("dp")
    order = sorted(range(n), key=lambda r: (r & 1, r))
    cut = [lax.dynamic_slice_in_dim(x, (me ^ r) * width, width, 1) for r in order]
    half = n // 2
    return jnp.concatenate(cut[:half], axis=1), jnp.concatenate(cut[half:], axis=1)


def scatter_dp(keep, send, rows):
    n = lax.axis_size("dp")
    half = n // 2
    steps = half.bit_length() - 1
    cols = keep.shape[1]
    moved = swap(send, 1)
    shape = (2,) * steps + (2, rows // 2, cols)
    keep = keep.reshape(shape)
    moved = moved.reshape(shape)
    done = []
    for color in range(2):
        cur = lax.index_in_dim(keep, color, steps, False).astype(F32) + lax.index_in_dim(
            moved, color, steps, False
        ).astype(F32)
        axes = list(range(steps))
        order = list(range(steps))
        if color == 0:
            order = order[::-1]
        for axis in order:
            at = axes.index(axis)
            away = lax.index_in_dim(cur, 1, at, False).astype(BF16)
            stay = lax.index_in_dim(cur, 0, at, False)
            bit = 1 << (steps - 1 - axis)
            cur = stay + swap(away, 2 * bit).astype(F32)
            axes.pop(at)
        done.append(cur)
    return jnp.concatenate(done, axis=0)


def scatter_dp_small(x):
    n = lax.axis_size("dp")
    bits = n.bit_length() - 1
    cur = x.reshape((2,) * bits + x.shape[1:])
    for b in range(bits):
        cur = cur[0] + swap(cur[1], 1 << (bits - 1 - b))
    return cur


def gather_dp(x):
    n = lax.axis_size("dp")
    rows, cols = x.shape
    bits = n.bit_length() - 1
    upper = list(range(1, bits))
    tables = []
    for color in range(2):
        order = (upper if color == 0 else upper[::-1]) + [0]
        cur = x[:, color * (cols // 2) : (color + 1) * (cols // 2)]
        for bit in order:
            cur = jnp.concatenate([cur, swap(cur, 1 << bit)], axis=0)
        tables.append((cur, order))
    return tables


def pick_rows(tables, relative, local_row, rows):
    out = []
    for table, order in tables:
        place = jnp.zeros_like(relative)
        for step, bit in enumerate(order):
            place = place + (((relative >> bit) & 1) << step)
        out.append(table[place * rows + local_row])
    return jnp.concatenate(out, axis=1)


def body(
    tokens,
    cotangent,
    src_of,
    lengths,
    norm1_gain,
    w_in,
    conv_w,
    w_out,
    norm2_gain,
    w_gate,
    w_up,
    w_down,
):
    groups = lax.axis_size("dp")
    me = lax.axis_index("dp")
    tok_dev, quarter = tokens.shape
    width = w_in.shape[1]
    block = width // groups
    slot_count = 2 * tok_dev // groups
    slots = groups * slot_count
    ids = ring_ids()
    own = ids[0]
    col_start = own * quarter

    source = src_of // tok_dev
    local_row = src_of % tok_dev
    relative = source ^ me
    dealt_tokens = pick_rows(gather_dp(tokens), relative, local_row, tok_dev)
    full_tokens = gather_cols(dealt_tokens, ids)
    dealt_cot = pick_rows(gather_dp(cotangent), relative, local_row, tok_dev)
    full_cot = gather_cols(dealt_cot, ids)

    onehot = (source[:, None] == jnp.arange(groups, dtype=jnp.int32)[None, :]).astype(jnp.int32)
    before = jnp.cumsum(onehot, axis=0) - onehot
    slot_rank = jnp.sum(before * onehot, axis=1)
    slot_index = source * slot_count + slot_rank
    to_slot = slot_index[None, :] == jnp.arange(slots, dtype=jnp.int32)[:, None]
    request = jnp.sum(jnp.where(to_slot, local_row[None, :] + 1, 0), axis=1) - 1
    wanted = lax.all_to_all(
        request.reshape(groups, slot_count), "dp", split_axis=0, concat_axis=0, tiled=True
    ).reshape(-1)

    def give_back(cols):
        held = jnp.dot(to_slot.astype(BF16), cols.astype(BF16), preferred_element_type=F32)
        back = lax.all_to_all(
            held.astype(BF16).reshape(groups, slot_count, quarter),
            "dp",
            split_axis=0,
            concat_axis=0,
            tiled=True,
        ).reshape(slots, quarter)
        place = wanted[None, :] == jnp.arange(tok_dev, dtype=jnp.int32)[:, None]
        return jnp.dot(place.astype(BF16), back, preferred_element_type=F32)

    seq_len = lengths[0]
    starts = jnp.cumsum(seq_len) - seq_len
    positions = jnp.arange(tok_dev, dtype=jnp.int32)
    marks = jnp.any(positions[:, None] == starts[None, :], axis=1).astype(F32)
    earlier = jnp.concatenate([jnp.ones((1,), F32), marks[:-1]])
    first = (1.0 - marks)[:, None]
    second = first * (1.0 - earlier)[:, None]
    taps = conv_w.astype(F32)
    gain_two_cols = lax.dynamic_slice_in_dim(norm2_gain, col_start, quarter)
    gain_one_cols = lax.dynamic_slice_in_dim(norm1_gain, col_start, quarter)

    inputs = full_tokens.astype(F32)
    scale_one = lax.rsqrt(jnp.mean(inputs * inputs, axis=-1, keepdims=True) + EPS)
    normed_one = (inputs * scale_one * norm1_gain).astype(BF16)
    projected = jnp.einsum("td,kde->kte", normed_one, w_in, preferred_element_type=F32)
    b_gate = projected[0]
    c_gate = projected[1]
    values = projected[2]
    gated = b_gate * values
    gated_one = shifted(gated, 1) * first
    gated_two = shifted(gated, 2) * second
    convolved = taps[0] * gated_two + taps[1] * gated_one + taps[2] * gated
    mixed_in = (c_gate * convolved).astype(BF16)

    def branch_part(chunk):
        cut = lax.dynamic_slice_in_dim(w_out, chunk * quarter, quarter, 1)
        return jnp.dot(mixed_in, cut, preferred_element_type=F32)

    inputs_cols = dealt_tokens.astype(F32)
    resid = inputs_cols + scatter_cols(branch_part, ids)
    full_resid = gather_cols(resid.astype(BF16), ids).astype(F32)
    scale_two = lax.rsqrt(jnp.mean(full_resid * full_resid, axis=-1, keepdims=True) + EPS)
    normed_two = (full_resid * scale_two * norm2_gain).astype(BF16)
    gate = jnp.dot(normed_two, w_gate, preferred_element_type=F32)
    up_proj = jnp.dot(normed_two, w_up, preferred_element_type=F32)
    sigmoid_gate = jax.nn.sigmoid(gate)
    activated = gate * sigmoid_gate
    hidden = (activated * up_proj).astype(BF16)
    d_hidden = outer_cols(full_cot, w_down)
    d_gate = (d_hidden * up_proj * sigmoid_gate * (1.0 + gate * (1.0 - sigmoid_gate))).astype(
        BF16
    )
    d_up = (d_hidden * activated).astype(BF16)
    dots_two = jnp.sum(d_gate.astype(F32) * gate + d_up.astype(F32) * up_proj, axis=1)
    dots_two = total_tensor(dots_two.reshape(-1, 128)).reshape(-1, 1)

    def normed_two_part(chunk):
        cut_gate = lax.dynamic_slice_in_dim(w_gate, chunk * quarter, quarter, 0)
        cut_up = lax.dynamic_slice_in_dim(w_up, chunk * quarter, quarter, 0)
        return outer_cols(d_gate, cut_gate) + outer_cols(d_up, cut_up)

    d_normed_two = scatter_cols(normed_two_part, ids)
    d_resid = (
        dealt_cot.astype(F32)
        + scale_two * (gain_two_cols * d_normed_two)
        - resid * (scale_two * scale_two) * (dots_two / width)
    )
    d_branch = gather_cols(d_resid.astype(BF16), ids)

    def ffn_part(chunk):
        cut = lax.dynamic_slice_in_dim(w_down, chunk * quarter, quarter, 1)
        return jnp.dot(hidden, cut, preferred_element_type=F32)

    out_cols = resid + scatter_cols(ffn_part, ids)

    def weight_grad(pair, right):
        keep, send = pair
        send_out = inner_rows(send, right).astype(BF16)
        keep_out = inner_rows(keep, right).astype(BF16)
        return scatter_dp(keep_out, send_out, block)

    cot_pair = relative_blocks(full_cot, me, block)
    normed_two_pair = relative_blocks(normed_two, me, block)
    down_out = weight_grad(cot_pair, hidden).T
    gate_out = weight_grad(normed_two_pair, d_gate)
    up_out = weight_grad(normed_two_pair, d_up)

    d_mixed = outer_cols(d_branch, w_out)
    d_conv = d_mixed * c_gate
    taps_grad = jnp.stack(
        [
            jnp.sum(d_conv * gated_two, axis=0),
            jnp.sum(d_conv * gated_one, axis=0),
            jnp.sum(d_conv * gated, axis=0),
        ]
    )
    d_gated = (
        taps[2] * d_conv
        + taps[1] * raised(d_conv * first, 1)
        + taps[0] * raised(d_conv * second, 2)
    )
    d_b = (d_gated * values).astype(BF16)
    d_c = (d_mixed * convolved).astype(BF16)
    d_values = (d_gated * b_gate).astype(BF16)
    d_proj = jnp.stack([d_b, d_c, d_values])
    dots_one = jnp.sum(
        d_b.astype(F32) * b_gate + d_c.astype(F32) * c_gate + d_values.astype(F32) * values, axis=1
    )
    dots_one = total_tensor(dots_one.reshape(-1, 128)).reshape(-1, 1)

    def normed_one_part(chunk):
        cut = lax.dynamic_slice_in_dim(w_in, chunk * quarter, quarter, 1)
        return jnp.einsum("kte,kde->td", d_proj, cut, preferred_element_type=F32)

    d_normed_one = scatter_cols(normed_one_part, ids)
    d_inputs = (
        d_resid
        + scale_one * (gain_one_cols * d_normed_one)
        - inputs_cols * (scale_one * scale_one) * (dots_one / width)
    )

    branch_pair = relative_blocks(d_branch, me, block)
    normed_one_pair = relative_blocks(normed_one, me, block)
    out_out = weight_grad(branch_pair, mixed_in).T
    d_proj_cols = jnp.concatenate([d_b, d_c, d_values], axis=1)
    in_out = weight_grad(normed_one_pair, d_proj_cols)
    in_out = jnp.stack([in_out[:, k * quarter : (k + 1) * quarter] for k in range(3)])
    tap_block = quarter // groups
    tap_parts = jnp.stack(
        [
            lax.dynamic_slice_in_dim(taps_grad, (me ^ r) * tap_block, tap_block, 1)
            for r in range(groups)
        ]
    )
    taps_out = scatter_dp_small(tap_parts)

    def rows_of(weight, axis):
        return lax.dynamic_slice_in_dim(weight, me * block, block, axis).astype(F32)

    gain_two_part = jnp.sum(rows_of(w_gate, 0) * gate_out + rows_of(w_up, 0) * up_out, axis=1)
    gain_one_part = jnp.sum(rows_of(w_in, 1) * in_out, axis=(0, 2))
    gains = total_tensor(jnp.stack([gain_one_part, gain_two_part]))
    gain_one_out = gains[0] / lax.dynamic_slice_in_dim(norm1_gain, me * block, block)
    gain_two_out = gains[1] / lax.dynamic_slice_in_dim(norm2_gain, me * block, block)

    mixed = give_back(out_cols)
    token_grad = give_back(d_inputs)
    return (
        mixed,
        token_grad,
        gain_one_out,
        in_out,
        taps_out,
        out_out,
        gain_two_out,
        gate_out,
        up_out,
        down_out,
    )


def solution(mesh):
    placed = (
        P("dp", "tensor"),
        P("dp", "tensor"),
        P("dp"),
        P("dp", None),
        P(),
        P(None, None, "tensor"),
        P(None, "tensor"),
        P("tensor", None),
        P(),
        P(None, "tensor"),
        P(None, "tensor"),
        P("tensor", None),
    )
    return jax.shard_map(
        body,
        mesh=mesh,
        in_specs=placed,
        out_specs=(
            P("dp", "tensor"),
            P("dp", "tensor"),
            P("dp"),
            P(None, "dp", "tensor"),
            P(None, ("tensor", "dp")),
            P("tensor", "dp"),
            P("dp"),
            P("dp", "tensor"),
            P("dp", "tensor"),
            P("tensor", "dp"),
        ),
        check_vma=False,
    )
```

```python
import jax
import jax.numpy as jnp
import numpy as np
from jax import lax
from jax.experimental import pallas as pl
from jax.experimental.pallas import tpu as pltpu
from jax.sharding import PartitionSpec as P

EPS = 1e-05
F32 = jnp.float32
BF16 = jnp.bfloat16
I32 = jnp.int32
ANY = pl.BlockSpec(memory_space=pl.ANY)


def dot(left, right, left_dim, right_dim):
    return lax.dot_general(
        left, right, (((left_dim,), (right_dim,)), ((), ())), preferred_element_type=F32
    )


def room(mebibytes):
    return pltpu.CompilerParams(vmem_limit_bytes=mebibytes << 20)


def shape(dims, dtype):
    return jax.ShapeDtypeStruct(tuple(dims), dtype)


def whole(dims):
    return pl.BlockSpec(tuple(dims), lambda *_: (0,) * len(dims))


def ring_order(n):
    return list(range(0, n, 2)) + list(range(1, n, 2))[::-1]


def ring_shift(x):
    n = lax.axis_size("tensor")
    order = ring_order(n)
    return lax.ppermute(x, "tensor", [(order[i], order[(i + 1) % n]) for i in range(n)])


def ring_ids():
    n = lax.axis_size("tensor")
    order = ring_order(n)
    place = {a: i for i, a in enumerate(order)}
    table = np.array(
        [[order[(place[a] - s) % n] for s in range(n)] for a in range(n)], np.int32
    )
    return jnp.asarray(table)[lax.axis_index("tensor")]


def gather_parts(x):
    parts = [x]
    for _ in range(1, lax.axis_size("tensor")):
        parts.append(ring_shift(parts[-1]))
    return parts


def total_direct(x):
    n = lax.axis_size("tensor")
    out = x
    for k in range(1, n):
        moved = lax.ppermute(x, "tensor", [(i, (i + k) % n) for i in range(n)])
        out = out + moved
    return out


def swap(x, mask):
    n = lax.axis_size("dp")
    return lax.ppermute(x, "dp", [(i, i ^ mask) for i in range(n)])


def gather_dp(x):
    n = lax.axis_size("dp")
    pieces = [None] * n
    for r in range(0, n, 2):
        pieces[r] = x if r == 0 else swap(x, r)
    for r in range(0, n, 2):
        pieces[r + 1] = swap(pieces[r], 1)
    return pieces


def scatter_dp_small(x):
    n = lax.axis_size("dp")
    bits = n.bit_length() - 1
    cur = x.reshape((2,) * bits + x.shape[1:])
    for b in range(bits):
        cur = cur[0] + swap(cur[1], 1 << (bits - 1 - b))
    return cur


def to_row(column):
    wide = jnp.broadcast_to(column, (column.shape[0], 128))
    return jnp.transpose(wide)[:8]


def to_column(row):
    return jnp.transpose(jnp.broadcast_to(row[:1], (8, row.shape[1])))[:, :1]


def one_hot(key, first, rows):
    at = lax.broadcasted_iota(I32, (key.shape[0], rows), 1) + first
    return jnp.where(at == key, 1.0, 0.0).astype(BF16)


def select_early_kernel(firsts, key_ref, *refs):
    pieces, out = refs[:-1], refs[-1]
    key = key_ref[...]
    acc = None
    for first, piece in zip(firsts, pieces):
        part = dot(one_hot(key, first, piece.shape[0]), piece[...], 1, 0)
        acc = part if acc is None else acc + part
    out[...] = acc


def select_late_kernel(firsts, key_ref, *refs):
    pieces, acc_ref, outs = refs[: len(firsts)], refs[len(firsts)], refs[len(firsts) + 1 :]
    key = key_ref[...]
    acc = acc_ref[...]
    for first, piece in zip(firsts, pieces):
        acc = acc + dot(one_hot(key, first, piece.shape[0]), piece[...], 1, 0)
    cols = outs[0].shape[1]
    for i, out in enumerate(outs[:-1]):
        out[...] = acc[:, i * cols : (i + 1) * cols].astype(BF16)
    outs[-1][...] = to_row(jnp.sum(acc * acc, axis=1, keepdims=True))


def select_rows(key, pieces, late):
    rows, cols = pieces[0].shape
    count = len(pieces) - late
    firsts = [r * rows for r in range(len(pieces))]
    acc = pl.pallas_call(
        lambda *refs: select_early_kernel(firsts[:count], *refs),
        out_shape=shape((key.shape[0], cols), F32),
        compiler_params=room(12),
    )(key, *pieces[:count])
    return pl.pallas_call(
        lambda *refs: select_late_kernel(firsts[count:], *refs),
        out_shape=[shape((key.shape[0], cols // 2), BF16)] * 2 + [shape((8, key.shape[0]), F32)],
        compiler_params=room(12),
    )(key, *pieces[count:], acc)


def hold_kernel(n, key_ref, *refs):
    parts, (out, hot_ref, cur_ref) = refs[:n], refs[-3:]
    step = pl.program_id(0)

    @pl.when(step == 0)
    def _():
        key = to_column(key_ref[...].astype(F32)).astype(I32)
        hot_ref[...] = one_hot(key, 0, hot_ref.shape[1])

    load_chunk(step, [[part] for part in parts], cur_ref)
    out[...] = dot(hot_ref[...], cur_ref[...], 1, 0).astype(BF16)


def hold_rows(key, parts, offset, count, before):
    n = len(parts)
    rows, cols = parts[0].shape
    before = [] if before is None else [before]
    return pl.pallas_call(
        lambda *refs: hold_kernel(n, *refs),
        grid=(n,),
        in_specs=[whole(key.shape)] + [whole((rows, cols))] * n + [ANY] * len(before),
        out_specs=pl.BlockSpec((key.shape[1], cols), lambda s: (0, s + offset)),
        out_shape=shape((key.shape[1], count * cols), BF16),
        scratch_shapes=[
            pltpu.VMEM((key.shape[1], rows), BF16),
            pltpu.VMEM((rows, cols), BF16),
        ],
        input_output_aliases={1 + n: 0} if before else {},
    )(key, *parts, *before)


def deal_kernel(n, block, info, key_ref, x_ref, out, own, mine_ref, other_ref, hot_ref):
    step = pl.program_id(0)

    @pl.when(step == 0)
    def _():
        key = to_column(key_ref[...].astype(F32)).astype(I32)
        hot_ref[...] = one_hot(key, 0, hot_ref.shape[1])

    dealt = dot(hot_ref[...], x_ref[...], 1, 0).astype(BF16)
    out[...] = dealt

    @pl.when(step == 0)
    def _():
        own[...] = dealt

    halves(
        lambda at: out[:, at : at + block],
        info[n],
        block,
        mine_ref.shape[0],
        mine_ref,
        other_ref,
    )


def deal_rows(info, key, x, half, block):
    n = lax.axis_size("tensor")
    rows = key.shape[1]
    slots, width = x.shape
    quarter = width // n
    half_spec = pl.BlockSpec((half // n, rows, block), lambda s, info: (info[s], 0, 0))
    half_shape = shape((half, rows, block), BF16)
    return pl.pallas_call(
        lambda *refs: deal_kernel(n, block, *refs),
        grid_spec=pltpu.PrefetchScalarGridSpec(
            num_scalar_prefetch=1,
            grid=(n,),
            in_specs=[whole(key.shape), pl.BlockSpec((slots, quarter), lambda s, info: (0, s))],
            out_specs=[
                pl.BlockSpec((rows, quarter), lambda s, info: (0, info[s])),
                whole((rows, quarter)),
                half_spec,
                half_spec,
            ],
            scratch_shapes=[pltpu.VMEM((rows, slots), BF16)],
        ),
        out_shape=[
            shape((rows, width), BF16),
            shape((rows, quarter), BF16),
            half_shape,
            half_shape,
        ],
    )(info, key, x)


def place_hot(key, rows):
    at = lax.broadcasted_iota(I32, (rows, key.shape[1]), 0)
    return jnp.where(at == key, 1.0, 0.0).astype(BF16)


def combine_kernel(groups, key_ref, *refs):
    out, hot_ref = refs[-2:]
    hot_ref[...] = place_hot(key_ref[...], out.shape[0])
    at = 0
    for i, (combine, ins) in enumerate(groups):
        x = combine(*[r[...].astype(F32) for r in refs[at : at + len(ins)]]).astype(BF16)
        cols = x.shape[1]
        out[:, i * cols : (i + 1) * cols] = dot(hot_ref[...], x, 1, 0).astype(BF16)
        at += len(ins)


def combine_rows(key, rows, groups, cols):
    ins = sum((list(i) for _, i in groups), [])
    return pl.pallas_call(
        lambda *refs: combine_kernel(groups, *refs),
        out_shape=shape((rows, cols), BF16),
        scratch_shapes=[pltpu.VMEM((rows, key.shape[1]), BF16)],
    )(key, *ins)


def place_kernel(key_ref, x_ref, *refs):
    outs, hot_ref = refs[:-1], refs[-1]
    hot_ref[...] = place_hot(key_ref[...], outs[0].shape[0])
    cols = outs[0].shape[1]
    for i, out in enumerate(outs):
        out[...] = dot(hot_ref[...], x_ref[:, i * cols : (i + 1) * cols], 1, 0)


def place_rows(key, x, rows, count):
    return pl.pallas_call(
        place_kernel,
        out_shape=[shape((rows, x.shape[1] // count), F32)] * count,
        scratch_shapes=[pltpu.VMEM((rows, key.shape[1]), BF16)],
    )(key, x)


def halves(read, core, block, count, mine_ref, other_ref):
    for i in range(count):
        low = read(2 * i * block)
        high = read((2 * i + 1) * block)
        mine_ref[i] = jnp.where(core == 0, low, high)
        other_ref[i] = jnp.where(core == 0, high, low)


def load_chunk(step, chunks, cur_ref):
    for k, pieces in enumerate(chunks):

        @pl.when(step == k)
        def _():
            at = 0
            for piece in pieces:
                cur_ref[:, at : at + piece.shape[1]] = piece[...]
                at += piece.shape[1]


def squares(chunks):
    total = None
    for pieces in chunks:
        for piece in pieces:
            x = piece[...].astype(F32)
            part = jnp.sum(x * x, axis=1, keepdims=True)
            total = part if total is None else total + part
    return total


def grouped(refs, chunks):
    out, at = [], 0
    for pieces in chunks:
        out.append(refs[at : at + len(pieces)])
        at += len(pieces)
    return out, refs[at:]


def not_first(info, at, rows):
    row = lax.broadcasted_iota(I32, (rows, 1), 0)
    first = jnp.ones((rows, 1), F32)
    second = first
    for k in range(at, info.shape[0]):
        first = jnp.where(row == info[k], 0.0, first)
        second = jnp.where((row == info[k]) | (row == info[k] + 1), 0.0, second)
    return first, second


def front_kernel(chunks, n, block, last, info, *refs):
    grid = len(chunks)
    chunks, refs = grouped(refs, chunks)
    step = pl.program_id(0)
    if last:
        gain_ref, scale_ref, w_ref, acc_in, taps_ref, out_w, _, _ = refs[:8]
        bcv_ref, mixed_ref, mine_ref, other_ref = refs[8:12]
        parts, (acc_ref, cur_ref, prod_ref) = refs[12:-3], refs[-3:]
    else:
        gain_ref, scale_ref, w_ref, acc_ref, mine_ref, other_ref, cur_ref = refs
    quarter = cur_ref.shape[1]

    @pl.when(step == 0)
    def _():
        if last:
            acc_ref[...] = acc_in[...]
        else:
            acc_ref[...] = jnp.zeros_like(acc_ref)

    load_chunk(step, chunks, cur_ref)
    normed = (cur_ref[...].astype(F32) * to_column(scale_ref[...]) * gain_ref[...]).astype(BF16)
    cur_ref[...] = normed
    halves(
        lambda at: cur_ref[:, at : at + block],
        info[n],
        block,
        mine_ref.shape[0],
        mine_ref,
        other_ref,
    )
    for k in range(3):
        cols = slice(k * quarter, (k + 1) * quarter)
        acc_ref[:, cols] += dot(normed, w_ref[k], 1, 0)

    if last:

        @pl.when(step == grid - 1)
        def _():
            b_gate = acc_ref[:, :quarter]
            c_gate = acc_ref[:, quarter : 2 * quarter]
            values = acc_ref[:, 2 * quarter :]
            bcv_ref[0] = b_gate
            bcv_ref[1] = c_gate
            bcv_ref[2] = values
            gated = b_gate * values
            first, second = not_first(info, n + 1, gated.shape[0])
            convolved = (
                taps_ref[0:1] * (pltpu.roll(gated, 2, 0) * second)
                + taps_ref[1:2] * (pltpu.roll(gated, 1, 0) * first)
                + taps_ref[2:3] * gated
            )
            mixed = (c_gate * convolved).astype(BF16)
            mixed_ref[...] = mixed
            prod_ref[...] = dot(mixed, out_w[...], 1, 0)
            write_parts(info, n, prod_ref, parts)


EXTRA = 16


def put_row(part, rows, row):
    part[rows:] = jnp.concatenate([row] * (EXTRA // 8), axis=0).astype(part.dtype)


def write_parts(info, n, prod_ref, parts):
    rows = prod_ref.shape[0]
    pieces = len(parts) // n
    cols = parts[0].shape[1]
    for s in range(n):
        for i in range(pieces):
            at = pl.multiple_of(info[s] * (cols * pieces) + i * cols, cols)
            part = parts[s * pieces + i]
            part[:rows] = prod_ref[:, pl.ds(at, cols)].astype(part.dtype)


def part_shapes(rows, n, pieces, cols):
    return [shape((rows, cols), F32 if s == 0 else BF16) for s in range(n) for _ in range(pieces)]


def front(info, chunks, gain, scale, w_in, half, block, offset, before=None, conv=None):
    n = lax.axis_size("tensor")
    rows = chunks[0][0].shape[0]
    quarter = w_in.shape[2]
    count = half // n
    flat = sum(chunks, [])
    last = before is not None
    in_specs = [whole(p.shape) for p in flat] + [
        pl.BlockSpec((1, quarter), lambda s, info: (0, info[s + offset])),
        whole((8, rows)),
        pl.BlockSpec((3, quarter, quarter), lambda s, info: (0, info[s + offset], 0)),
    ]
    half_spec = pl.BlockSpec((count, rows, block), lambda s, info: (info[s + offset], 0, 0))
    half_shape = shape((half, rows, block), BF16)
    wide = (rows, 3 * quarter)
    args = [info, *flat, gain[None, :], scale, w_in]
    aliases = {}
    scratch = [pltpu.VMEM((rows, quarter), BF16)]
    if last:
        acc, mine, other = before
        taps, w_out = conv
        in_specs += [whole(wide), whole((3, quarter)), whole(w_out.shape), ANY, ANY]
        args += [acc, taps, w_out, mine, other]
        extra = part_shapes(rows, n, 2, quarter // 2)
        out_specs = [whole((3, rows, quarter)), whole((rows, quarter))]
        out_shape = [shape((3, rows, quarter), F32), shape((rows, quarter), BF16)]
        aliases = {len(args) - 2: 2, len(args) - 1: 3}
        scratch = [pltpu.VMEM(wide, F32)] + scratch + [pltpu.VMEM((rows, n * quarter), F32)]
    else:
        extra = []
        out_specs = [whole(wide)]
        out_shape = [shape(wide, F32)]
    return pl.pallas_call(
        lambda *refs: front_kernel(chunks, n, block, last, *refs),
        grid_spec=pltpu.PrefetchScalarGridSpec(
            num_scalar_prefetch=1,
            grid=(len(chunks),),
            in_specs=in_specs,
            out_specs=out_specs + [half_spec, half_spec] + [whole(e.shape) for e in extra],
            scratch_shapes=scratch,
        ),
        out_shape=out_shape + [half_shape, half_shape] + extra,
        input_output_aliases=aliases,
    )(*args)


def ffn_kernel(chunks, n, half, block, steps, info, *refs):
    chunks, refs = grouped(refs, chunks)
    cot_ref, gain_ref, gate_w, up_w, down_w = refs[:5]
    hidden_ref, d_gate_ref, d_up_ref, scale_ref, mine_ref, other_ref = refs[5:11]
    parts, (normed_ref, acc_ref, sums_ref) = refs[11:-3], refs[-3:]
    width = normed_ref.shape[1]
    quarter = width // n
    step = pl.program_id(0)

    @pl.when(step == 0)
    def _():
        scale = lax.rsqrt(squares(chunks) / width + EPS)
        scale_ref[...] = scale
        for k in range(n):
            start = info[k] * quarter
            for piece in chunks[k]:
                cols = piece.shape[1]
                at = pl.ds(pl.multiple_of(start, cols), cols)
                normed_ref[:, at] = (piece[...].astype(F32) * scale * gain_ref[:, at]).astype(BF16)
                start = start + cols
        halves(
            lambda at: normed_ref[:, at : at + block], info[n], block, half, mine_ref, other_ref
        )

    normed = normed_ref[...]
    gate = dot(normed, gate_w[...], 1, 0)
    up_proj = dot(normed, up_w[...], 1, 0)
    d_hidden = dot(cot_ref[...], down_w[...], 1, 1)
    sigmoid_gate = jax.nn.sigmoid(gate)
    activated = gate * sigmoid_gate
    hidden_ref[...] = (activated * up_proj).astype(BF16)
    d_gate = d_hidden * up_proj * sigmoid_gate * (1.0 + gate * (1.0 - sigmoid_gate))
    d_up = d_hidden * activated
    sums = jnp.sum(d_gate * gate + d_up * up_proj, axis=1, keepdims=True)
    d_gate = d_gate.astype(BF16)
    d_up = d_up.astype(BF16)
    d_gate_ref[...] = d_gate
    d_up_ref[...] = d_up
    back_prod = dot(d_gate, gate_w[...], 1, 1) + dot(d_up, up_w[...], 1, 1)

    @pl.when(step == 0)
    def _():
        acc_ref[...] = back_prod
        sums_ref[...] = sums

    @pl.when(step > 0)
    def _():
        acc_ref[...] += back_prod
        sums_ref[...] += sums

    @pl.when(step == steps - 1)
    def _():
        write_parts(info, n, acc_ref, parts)
        row = to_row(sums_ref[...])
        for part in parts:
            put_row(part, acc_ref.shape[0], row)


def ffn(info, chunks, cot, gain, w_gate, w_up, w_down, half, block):
    n = len(chunks)
    flat = sum(chunks, [])
    rows = flat[0].shape[0]
    width, units = w_gate.shape
    step = 512
    parts = part_shapes(rows + EXTRA, n, 1, width // n)
    return pl.pallas_call(
        lambda *refs: ffn_kernel(chunks, n, half, block, units // step, *refs),
        grid_spec=pltpu.PrefetchScalarGridSpec(
            num_scalar_prefetch=1,
            grid=(units // step,),
            in_specs=[whole(p.shape) for p in flat]
            + [
                whole((rows, width)),
                whole((1, width)),
                pl.BlockSpec((width, step), lambda j, info: (0, j)),
                pl.BlockSpec((width, step), lambda j, info: (0, j)),
                pl.BlockSpec((step, width), lambda j, info: (j, 0)),
            ],
            out_specs=[pl.BlockSpec((rows, step), lambda j, info: (0, j))] * 3
            + [whole((rows, 1))]
            + [whole((half, rows, block))] * 2
            + [whole(p.shape) for p in parts],
            scratch_shapes=[
                pltpu.VMEM((rows, width), BF16),
                pltpu.VMEM((rows, width), F32),
                pltpu.VMEM((rows, 1), F32),
            ],
        ),
        out_shape=[shape((rows, units), BF16)] * 3
        + [shape((rows, 1), F32)]
        + [shape((half, rows, block), BF16)] * 2
        + parts,
    )(info, *flat, cot, gain[None, :], w_gate, w_up, w_down)


def mix_kernel(chunks, block, core_at, info, *refs):
    w_ref, acc_ref, mine_ref, other_ref, cur_ref = refs[len(chunks) :]
    step = pl.program_id(0)
    load_chunk(step, [[ref] for ref in refs[: len(chunks)]], cur_ref)
    halves(
        lambda at: cur_ref[:, at : at + block],
        info[core_at],
        block,
        mine_ref.shape[0],
        mine_ref,
        other_ref,
    )

    @pl.when(step == 0)
    def _():
        acc_ref[...] = jnp.zeros_like(acc_ref)

    acc_ref[...] += dot(cur_ref[...], w_ref[...], 1, 1)


def mix_back(info, chunks, w_out, half, block):
    n = lax.axis_size("tensor")
    rows, quarter = chunks[0].shape
    half_spec = pl.BlockSpec((half // n, rows, block), lambda s, info: (info[s], 0, 0))
    half_shape = shape((half, rows, block), BF16)
    return pl.pallas_call(
        lambda *refs: mix_kernel(chunks, block, n, *refs),
        grid_spec=pltpu.PrefetchScalarGridSpec(
            num_scalar_prefetch=1,
            grid=(len(chunks),),
            in_specs=[whole((rows, quarter))] * len(chunks)
            + [pl.BlockSpec((quarter, quarter), lambda s, info: (0, info[s]))],
            out_specs=[whole((rows, quarter)), half_spec, half_spec],
            scratch_shapes=[pltpu.VMEM((rows, quarter), BF16)],
        ),
        out_shape=[shape((rows, quarter), F32), half_shape, half_shape],
    )(info, *chunks, w_out)


def back_kernel(n, block, info, *refs):
    chunk, out_w, in_w, acc_ref, bcv_ref, taps_ref = refs[:6]
    proj_ref, taps_grad_ref, mine_ref, other_ref = refs[8:12]
    parts = refs[12:]
    step = pl.program_id(0)
    rows, quarter = chunk.shape

    @pl.when(step == 0)
    def _():
        halves(
            lambda at: chunk[:, at : at + block],
            info[n],
            block,
            mine_ref.shape[0],
            mine_ref,
            other_ref,
        )
        d_mixed = acc_ref[...] + dot(chunk[...], out_w[...], 1, 1)
        b_gate, c_gate, values = bcv_ref[0], bcv_ref[1], bcv_ref[2]
        first, second = not_first(info, n + 1, rows)
        gated = b_gate * values
        gated_one = pltpu.roll(gated, 1, 0) * first
        gated_two = pltpu.roll(gated, 2, 0) * second
        convolved = taps_ref[0:1] * gated_two + taps_ref[1:2] * gated_one + taps_ref[2:3] * gated
        d_conv = d_mixed * c_gate
        taps_grad_ref[0:1] = jnp.sum(d_conv * gated_two, axis=0, keepdims=True)
        taps_grad_ref[1:2] = jnp.sum(d_conv * gated_one, axis=0, keepdims=True)
        taps_grad_ref[2:3] = jnp.sum(d_conv * gated, axis=0, keepdims=True)
        d_gated = (
            taps_ref[2:3] * d_conv
            + taps_ref[1:2] * pltpu.roll(d_conv * first, rows - 1, 0)
            + taps_ref[0:1] * pltpu.roll(d_conv * second, rows - 2, 0)
        )
        dots = None
        for k, (grad, value) in enumerate(
            ((d_gated * values, b_gate), (d_mixed * convolved, c_gate), (d_gated * b_gate, values))
        ):
            proj_ref[:, k * quarter : (k + 1) * quarter] = grad.astype(BF16)
            part = jnp.sum(grad * value, axis=1, keepdims=True)
            dots = part if dots is None else dots + part
        for part in parts:
            put_row(part, rows, to_row(dots))

    for s in range(n):

        @pl.when(step == 1 + s)
        def _():
            part = parts[(s + 1) % n]
            total = None
            for k in range(3):
                cols = slice(k * quarter, (k + 1) * quarter)
                prod = dot(proj_ref[:, cols], in_w[k], 1, 1)
                total = prod if total is None else total + prod
            part[:rows] = total.astype(part.dtype)


def back(info, chunk, before, w_out, w_in, bcv, taps, half, block):
    n = lax.axis_size("tensor")
    rows, quarter = chunk.shape
    acc, mine, other = before
    half_spec = pl.BlockSpec((half // n, rows, block), lambda s, info: (info[n - 1], 0, 0))

    def late(s):
        turn = jnp.maximum(s, 1)
        return jnp.where(turn == n, 0, turn)

    parts = part_shapes(rows + EXTRA, n, 1, quarter)
    return pl.pallas_call(
        lambda *refs: back_kernel(n, block, *refs),
        grid_spec=pltpu.PrefetchScalarGridSpec(
            num_scalar_prefetch=1,
            grid=(1 + n,),
            in_specs=[
                whole((rows, quarter)),
                pl.BlockSpec((quarter, quarter), lambda s, info: (0, info[n - 1])),
                pl.BlockSpec((3, quarter, quarter), lambda s, info: (0, info[late(s)], 0)),
                whole((rows, quarter)),
                whole((3, rows, quarter)),
                whole((3, quarter)),
                ANY,
                ANY,
            ],
            out_specs=[
                whole((rows, 3 * quarter)),
                whole((3, quarter)),
                half_spec,
                half_spec,
            ]
            + [whole(p.shape) for p in parts],
        ),
        out_shape=[
            shape((rows, 3 * quarter), BF16),
            shape((3, quarter), F32),
            shape((half, rows, block), BF16),
            shape((half, rows, block), BF16),
        ]
        + parts,
        input_output_aliases={7: 2, 8: 3},
    )(info, chunk, w_out, w_in, acc, bcv, taps, mine, other)


def ring_sum(parts):
    n = len(parts)
    acc = parts[1 % n].astype(BF16)
    for s in range(1, n):
        moved = ring_shift(acc)
        if s < n - 1:
            acc = (moved.astype(F32) + parts[s + 1].astype(F32)).astype(BF16)
    return moved, parts[0]


def weight_tables(half):
    steps = half.bit_length() - 1
    bits = [0, steps - 1]
    order = sorted(range(half), key=lambda j: -sum((j >> b) & 1 for b in bits))

    def without(j, b):
        return (j & ((1 << b) - 1)) | ((j >> (b + 1)) << b)

    tables = []
    for sent in (1, 0):
        for b in bits:
            at = [without(j, b) if (j >> b) & 1 == sent else None for j in order]
            held = next(a for a in at if a is not None)
            row = []
            for a in at:
                held = held if a is None else a
                row.append(held)
            tables.append(row)
    return bits, order, tables


def weight_kernel(terms, bits, half, info, *refs):
    ins, outs = refs[: 4 * terms], refs[4 * terms : 4 * terms + 4]
    held, sems = refs[4 * terms + 4 :]
    step = pl.program_id(0)
    slot = step % 2
    j = info[1 + step]
    rows = outs[0].shape[1]

    def copy(at, color, out, block):
        source = held.at[at, pl.ds(color * rows, rows)]
        return pltpu.make_async_copy(source, outs[out].at[block], sems.at[at, color])

    @pl.when(step >= 2)
    def _():
        for color in range(2):
            copy(slot, color, color, 0).wait()

    at = 0
    for t in range(terms):
        x_own, x_far, z_own, z_far = ins[4 * t : 4 * t + 4]
        cols = z_own.shape[1]
        grad = dot(x_own[0], z_own[...], 0, 0) + dot(x_far[0], z_far[...], 0, 0)
        held[slot, :, at : at + cols] = grad.astype(BF16)
        at += cols
    for color in range(2):
        away = (j >> bits[color]) & 1
        for out, mine in ((color, away == 1), (2 + color, away == 0)):

            @pl.when(mine)
            def _():
                copy(slot, color, out, info[1 + half + out * half + step]).start()

    @pl.when(step == half - 1)
    def _():
        for color in range(2):
            copy(slot, color, color, 0).wait()
            if half > 1:
                copy(1 - slot, color, color, 0).wait()


def weight_grads(terms, half):
    me = lax.axis_index("dp")
    bits, order, tables = weight_tables(half)
    flat = np.array(order + sum(tables, []), np.int32)
    info = jnp.concatenate([(me >> 1)[None].astype(I32), jnp.asarray(flat)])
    block = terms[0][0].shape[2]
    rows = terms[0][0].shape[1]
    cols = sum(t[2].shape[1] for t in terms)
    in_specs = []
    args = []
    for x_own, x_far, z_own, z_far in terms:
        x_spec = pl.BlockSpec((1, rows, block), lambda g, info: (info[1 + g] ^ info[0], 0, 0))
        in_specs += [x_spec, x_spec, whole(z_own.shape), whole(z_far.shape)]
        args += [x_own, x_far, z_own, z_far]

    return pl.pallas_call(
        lambda *refs: weight_kernel(len(terms), bits, half, *refs),
        grid_spec=pltpu.PrefetchScalarGridSpec(
            num_scalar_prefetch=1,
            grid=(half,),
            in_specs=in_specs,
            out_specs=[ANY] * 4,
            scratch_shapes=[
                pltpu.VMEM((2, block, cols), BF16),
                pltpu.SemaphoreType.DMA((2, 2)),
            ],
        ),
        out_shape=[shape((half // 2, block // 2, cols), BF16)] * 4,
    )(info, *args)


def add_kernel(*refs):
    ins, outs = refs[:4], refs[4:]
    for color, out in enumerate(outs):
        keep, moved = ins[2 * color : 2 * color + 2]
        out[...] = (keep[0].astype(F32) + moved[0].astype(F32)).astype(BF16)


def scatter_pair(grads):
    moved = [swap(grads[color], 2 << color) for color in range(2)]
    _, rows, cols = grads[0].shape
    step = cols // 2
    spec = pl.BlockSpec((1, rows, step), lambda j: (1, 0, j))
    go = pl.pallas_call(
        add_kernel,
        grid=(cols // step,),
        in_specs=[spec] * 4,
        out_specs=[pl.BlockSpec((rows, step), lambda j: (0, j))] * 2,
        out_shape=[shape((rows, cols), BF16)] * 2,
    )(grads[2], moved[0], grads[3], moved[1])
    return [[grads[2 + color], moved[color], swap(go[color], 4 >> color)] for color in range(2)]


def scatter_rest(grads, half):
    steps = half.bit_length() - 1
    if steps == 2:
        return scatter_pair(grads)
    bits = [0, steps - 1]
    done = []
    for color in range(2):
        away, stay = grads[color], grads[2 + color]
        first = bits[color]
        left = [b for b in range(steps) if b != first]
        inner = stay.shape[1:]
        view = (2,) * len(left) + inner
        moved = swap(away, 2 << first)
        held = [stay.reshape(view), moved.reshape(view)]
        kept = list(held)
        axes = left[::-1]
        for b in left if color == 0 else left[::-1]:
            at = axes.index(b)
            go = sum(lax.index_in_dim(h, 1, at, False).astype(F32) for h in held)
            go = go.astype(BF16)
            held = [lax.index_in_dim(h, 0, at, False) for h in held]
            held.append(swap(go, 2 << b))
            kept.append(held[-1])
            axes.pop(at)
        done.append(kept)
    return done


def summed(rows, counts):
    halves_of, at = [], 0
    for count in counts:
        total = None
        for h in rows[at : at + count]:
            x = h[...].reshape(h.shape[-2:]).astype(F32)
            total = x if total is None else total + x
        halves_of.append(total)
        at += count
    return jnp.concatenate(halves_of, axis=0)


def held_specs(rows, step, place=lambda j: j):
    args, specs, counts = [], [], []
    for held in rows:
        counts.append(len(held))
        for h in held:
            lead = len(h.shape) - 2
            args.append(h)
            specs.append(
                pl.BlockSpec(
                    (1,) * lead + (h.shape[-2], step), lambda j, *_, lead=lead: (0,) * lead + (0, place(j))
                )
            )
    return args, specs, counts


def end_down(rows, units, block, step):
    args, specs, counts = held_specs(rows, step)

    def kernel(*refs):
        refs[-1][...] = jnp.transpose(summed(refs[:-1], counts))

    return pl.pallas_call(
        kernel,
        grid=(units // step,),
        in_specs=specs,
        out_specs=pl.BlockSpec((step, block), lambda j: (j, 0)),
        out_shape=shape((units, block), F32),
    )(*args)


def end_gains(sets, weights, weight_specs, gain, outs, out_specs, turns, grid, block):
    me = lax.axis_index("dp")
    args = sum((list(held) for held, _, _ in sets), [])
    specs = sum((held_specs for _, held_specs, _ in sets), [])

    def kernel(info, *refs):
        held, rest = refs[: len(args)], refs[len(args) :]
        weight_refs, gain_ref = rest[: len(weights)], rest[len(weights)]
        out_refs, gain_out, acc = rest[len(weights) + 1 : -2], rest[-2], rest[-1]
        j = pl.program_id(0)

        @pl.when(j == 0)
        def _():
            acc[...] = jnp.zeros_like(acc)

        for when, index, weight, out, flip in turns:
            at = sum(len(h) for h, _, _ in sets[:index])

            @pl.when(when(j))
            def _():
                total = summed(held[at : at + len(sets[index][0])], sets[index][2])
                out_ref = out_refs[out]
                out_ref[...] = (jnp.transpose(total) if flip else total).reshape(out_ref.shape)
                if weight is not None:
                    w = weight_refs[weight][...].reshape(total.shape).astype(F32)
                    acc[...] += jnp.sum(total * w, axis=1, keepdims=True)

        @pl.when(j == grid - 1)
        def _():
            gain_out[...] = to_row(acc[...]) / gain_ref[...]

    return pl.pallas_call(
        kernel,
        grid_spec=pltpu.PrefetchScalarGridSpec(
            num_scalar_prefetch=1,
            grid=(grid,),
            in_specs=specs + weight_specs + [whole((1, block))],
            out_specs=out_specs + [whole((8, block))],
            scratch_shapes=[pltpu.VMEM((block, 1), F32)],
        ),
        out_shape=outs + [shape((8, block), F32)],
    )(me[None].astype(I32), *args, *weights, gain)


def end_both(gate_rows, up_rows, w_gate, w_up, gain, units, block, step):
    count = units // step
    first = lambda j: jnp.minimum(j, count - 1)
    second = lambda j: jnp.maximum(j - count, 0)
    return end_gains(
        [held_specs(gate_rows, step, first), held_specs(up_rows, step, second)],
        [w_gate, w_up],
        [
            pl.BlockSpec((block, step), lambda j, info: (info[0], first(j))),
            pl.BlockSpec((block, step), lambda j, info: (info[0], second(j))),
        ],
        gain,
        [shape((block, units), F32)] * 2,
        [
            pl.BlockSpec((block, step), lambda j, info: (0, first(j))),
            pl.BlockSpec((block, step), lambda j, info: (0, second(j))),
        ],
        [(lambda j: j < count, 0, 0, 0, False), (lambda j: j >= count, 1, 1, 1, False)],
        2 * count,
        block,
    )


def end_late(rows, w_in, gain, block, quarter):
    first = lambda j: jnp.minimum(j, 2)
    return end_gains(
        [held_specs(rows, quarter)],
        [w_in],
        [pl.BlockSpec((1, block, quarter), lambda j, info: (first(j), info[0], 0))],
        gain,
        [shape((3, block, quarter), F32), shape((quarter, block), F32)],
        [
            pl.BlockSpec((1, block, quarter), lambda j, info: (first(j), 0, 0)),
            whole((quarter, block)),
        ],
        [(lambda j: j < 3, 0, 0, 0, False), (lambda j: j == 3, 0, None, 1, True)],
        4,
        block,
    )


def body(
    tokens,
    cotangent,
    src_of,
    lengths,
    norm1_gain,
    w_in,
    conv_w,
    w_out,
    norm2_gain,
    w_gate,
    w_up,
    w_down,
):
    groups = lax.axis_size("dp")
    n = lax.axis_size("tensor")
    half = groups // 2
    me = lax.axis_index("dp")
    tok_dev, quarter = tokens.shape
    width = w_in.shape[1]
    units = w_gate.shape[1]
    block = width // groups
    slot_count = 2 * tok_dev // groups
    slots = groups * slot_count
    ids = ring_ids()
    seq_len = lengths[0]
    starts = jnp.cumsum(seq_len) - seq_len
    info = jnp.concatenate([ids, (me & 1)[None].astype(I32), starts.astype(I32)])
    col_start = ids[0] * quarter

    source = src_of // tok_dev
    local_row = src_of % tok_dev
    key = ((source ^ me) * tok_dev + local_row)[:, None]

    onehot = (source[:, None] == jnp.arange(groups, dtype=I32)[None, :]).astype(I32)
    before = jnp.cumsum(onehot, axis=0) - onehot
    slot_rank = jnp.sum(before * onehot, axis=1)
    slot_index = source * slot_count + slot_rank
    to_slot = slot_index[None, :] == jnp.arange(slots, dtype=I32)[:, None]
    request = jnp.sum(jnp.where(to_slot, local_row[None, :] + 1, 0), axis=1) - 1
    wanted = lax.all_to_all(
        request.reshape(groups, slot_count), "dp", split_axis=0, concat_axis=0, tiled=True
    ).reshape(-1)

    def exchange(held):
        rows = lax.all_to_all(
            held.reshape(groups, slot_count, held.shape[1]),
            "dp",
            split_axis=0,
            concat_axis=0,
            tiled=True,
        )
        return rows.reshape(slots, held.shape[1])


    def give_back(combine, ins):
        held = combine_rows(slot_index[None, :], slots, [(combine, ins)], quarter)
        return place_rows(wanted[None, :], exchange(held), tok_dev, 1)[0]

    *token_halves, squares_own = select_rows(key, gather_dp(tokens), groups // 2)
    squares_all = total_direct(squares_own)
    scale_one = lax.rsqrt(squares_all / width + EPS)
    token_a = gather_parts(token_halves[0])
    token_b = gather_parts(token_halves[1])
    token_parts = [[a, b] for a, b in zip(token_a, token_b)]

    cot_parts = gather_parts(cotangent)
    held_cot = hold_rows(wanted[None, :], cot_parts[:-1], 0, n, None)
    held_cot = hold_rows(wanted[None, :], cot_parts[-1:], n - 1, n, held_cot)
    cot_slots = exchange(held_cot)
    cot, own_cot, cot_mine, cot_other = deal_rows(info, slot_index[None, :], cot_slots, half, block)

    taps = conv_w.astype(F32)

    def cut(gain, start, size):
        return lax.dynamic_slice_in_dim(gain, start, size)[None, :]

    one_cols = cut(norm1_gain, col_start, quarter)
    two_cols = cut(norm2_gain, col_start, quarter)
    one_rows = cut(norm1_gain, me * block, block)
    two_rows = cut(norm2_gain, me * block, block)

    split = n - 1
    so_far = front(info, token_parts[:split], norm1_gain, scale_one, w_in, half, block, 0)
    bcv, mixed_in, one_mine, one_other, *products = front(
        info,
        token_parts[split:],
        norm1_gain,
        scale_one,
        w_in,
        half,
        block,
        split,
        so_far,
        (taps, w_out),
    )
    resid = []
    resid_parts = []
    for i in range(2):
        moved, own_part = ring_sum(products[i::2])
        part = token_halves[i].astype(F32) + (moved.astype(F32) + own_part)
        resid.append(part)
        resid_parts.append(gather_parts(part.astype(BF16)))
    resid_parts = [list(p) for p in zip(*resid_parts)]

    one_far = swap(one_other, 1)
    mixed_far = swap(mixed_in, 1)
    cot_far = swap(cot_other, 1)
    hidden, d_gate, d_up, scale_two, two_mine, two_other, *products = ffn(
        info, resid_parts, cot, norm2_gain, w_gate, w_up, w_down, half, block
    )
    hidden_far = swap(hidden, 1)
    two_far = swap(two_other, 1)
    d_gate_far = swap(d_gate, 1)
    d_up_far = swap(d_up, 1)
    moved, own_part = ring_sum(products)
    total = moved.astype(F32) + own_part
    d_normed_two = total[:tok_dev]
    dots_two = total[tok_dev][:, None]
    resid_own = jnp.concatenate(resid, axis=1)
    d_resid = (
        own_cot.astype(F32)
        + scale_two * (two_cols * d_normed_two)
        - resid_own * (scale_two * scale_two) * (dots_two / width)
    )
    branch_parts = gather_parts(d_resid.astype(BF16))

    down_grads = weight_grads([(cot_mine, cot_far, hidden, hidden_far)], half)
    gate_grads = weight_grads([(two_mine, two_far, d_gate, d_gate_far)], half)
    up_grads = weight_grads([(two_mine, two_far, d_up, d_up_far)], half)
    down_rows = scatter_rest(down_grads, half)
    gate_rows = scatter_rest(gate_grads, half)
    up_rows = scatter_rest(up_grads, half)

    ffn_out = dot(hidden, w_down, 1, 0).astype(BF16)
    ffn_parts = [
        lax.dynamic_slice_in_dim(ffn_out, ids[s] * quarter, quarter, 1) for s in range(n)
    ]

    def block_out(moved, own_part, *res):
        return (moved + own_part) + jnp.concatenate(res, axis=1)

    ffn_ins = [*ring_sum(ffn_parts), *resid]
    mixed = give_back(block_out, ffn_ins)

    before = mix_back(info, branch_parts[:-1], w_out, half, block)
    d_proj, taps_grad, branch_mine, branch_other, *products = back(
        info, branch_parts[-1], before, w_out, w_in, bcv, taps, half, block
    )
    branch_far = swap(branch_other, 1)
    proj_far = swap(d_proj, 1)

    def input_grad(moved, own_part, d_res, scale, gain, *inputs):
        total = moved + own_part
        dots = jnp.transpose(total[tok_dev : tok_dev + 8])[:, :1]
        d_normed_one = total[:tok_dev]
        inputs = jnp.concatenate(inputs, axis=1)
        scale = to_column(scale)
        return d_res + scale * (gain * d_normed_one) - inputs * (scale * scale) * (dots / width)

    grad_ins = [
        *ring_sum(products),
        d_resid,
        scale_one,
        one_cols,
        *token_halves,
    ]
    token_grad = give_back(input_grad, grad_ins)

    late_grads = weight_grads(
        [
            (one_mine, one_far, d_proj, proj_far),
            (branch_mine, branch_far, mixed_in, mixed_far),
        ],
        half,
    )
    late_rows = scatter_rest(late_grads, half)
    tap_block = quarter // groups
    tap_parts = jnp.stack(
        [
            lax.dynamic_slice_in_dim(taps_grad, (me ^ r) * tap_block, tap_block, 1)
            for r in range(groups)
        ]
    )
    taps_out = scatter_dp_small(tap_parts)

    down_out = end_down(down_rows, units, block, 2 * quarter)
    gate_out, up_out, gain_two = end_both(
        gate_rows, up_rows, w_gate, w_up, two_rows, units, block, 2 * quarter
    )
    in_out, out_out, gain_one = end_late(
        late_rows, w_in, one_rows, block, quarter
    )
    gains = total_direct(jnp.concatenate([gain_one, gain_two], axis=1))[0]
    gain_one_out = gains[:block]
    gain_two_out = gains[block:]

    return (
        mixed,
        token_grad,
        gain_one_out,
        in_out,
        taps_out,
        out_out,
        gain_two_out,
        gate_out,
        up_out,
        down_out,
    )


def solution(mesh):
    placed = (
        P("dp", "tensor"),
        P("dp", "tensor"),
        P("dp"),
        P("dp", None),
        P(),
        P(None, None, "tensor"),
        P(None, "tensor"),
        P("tensor", None),
        P(),
        P(None, "tensor"),
        P(None, "tensor"),
        P("tensor", None),
    )

    return jax.shard_map(
        body,
        mesh=mesh,
        in_specs=placed,
        out_specs=(
            P("dp", "tensor"),
            P("dp", "tensor"),
            P("dp"),
            P(None, "dp", "tensor"),
            P(None, ("tensor", "dp")),
            P("tensor", "dp"),
            P("dp"),
            P("dp", "tensor"),
            P("dp", "tensor"),
            P("tensor", "dp"),
        ),
        check_vma=False,
    )
```
